32 devices in a mesh: rep: 4 (over y, x), shard: 8 (over z, core).
Axes of the slice: x: 2, y: 2, z: 4, core: 2. Of those that a mesh axis runs over, the one named last changes fastest.
Arguments:
- hidden_in: float32 [4096, 768], P(('rep', 'shard')), may hold values from -6 to 6
- doc_ids: int32 [32, 128], P(('rep', 'shard')), may hold values from 0 to 3, never falling along the last dimension, each value on 1 to 64 neighbouring positions
- cotangent: float32 [4096, 768], P(('rep', 'shard')), may hold values from -6 to 6
- pre_gain: float32 [1, 768], P(None, 'shard'), may hold values from 0.25 to 1.75
- pre_shift: float32 [1, 768], P(None, 'shard'), may hold values from -3 to 3
- qkv_weight: float32 [1, 768, 2304], P(None, 'shard'), may hold values from -0.21875 to 0.21875
- query_bias: float32 [1, 768], P(None, 'shard'), may hold values from -3 to 3
- value_bias: float32 [1, 768], P(None, 'shard'), may hold values from -3 to 3
- out_weight: float32 [1, 768, 768], P(None, 'shard'), may hold values from -0.875 to 0.875
- out_bias: float32 [1, 768], P(None, 'shard'), may hold values from -3 to 3
- post_gain: float32 [1, 768], P(None, 'shard'), may hold values from 0.25 to 1.75
- post_shift: float32 [1, 768], P(None, 'shard'), may hold values from -3 to 3
- up_weight: float32 [1, 768, 3072], P(None, 'shard'), may hold values from -0.21875 to 0.21875
- up_bias: float32 [1, 3072], P(None, 'shard'), may hold values from -3 to 3
- down_weight: float32 [1, 3072, 768], P(None, 'shard'), may hold values from -0.109375 to 0.109375
- down_bias: float32 [1, 768], P(None, 'shard'), may hold values from -3 to 3
Outputs:
- hidden_out: float32 [4096, 768], P(('rep', 'shard'))
- input_grad: float32 [4096, 768], P(('rep', 'shard'))
- grad_pre_gain: float32 [1, 768], P(None, 'shard')
- grad_pre_shift: float32 [1, 768], P(None, 'shard')
- grad_qkv_weight: float32 [1, 768, 2304], P(None, 'shard')
- grad_query_bias: float32 [1, 768], P(None, 'shard')
- grad_value_bias: float32 [1, 768], P(None, 'shard')
- grad_out_weight: float32 [1, 768, 768], P(None, 'shard')
- grad_out_bias: float32 [1, 768], P(None, 'shard')
- grad_post_gain: float32 [1, 768], P(None, 'shard')
- grad_post_shift: float32 [1, 768], P(None, 'shard')
- grad_up_weight: float32 [1, 768, 3072], P(None, 'shard')
- grad_up_bias: float32 [1, 3072], P(None, 'shard')
- grad_down_weight: float32 [1, 3072, 768], P(None, 'shard')
- grad_down_bias: float32 [1, 768], P(None, 'shard')
The draws below stay inside these ranges and needn't reach their ends.
Inputs may be any that keep to these rules, and one draw needn't show every extreme that they name: `doc_ids`: along each row the document number never falls; all 4 documents appear in every row, each of 1 to 64 tokens, one of exactly 64.
All inputs are finite; a program needn't handle non-finite values.
Results may differ from the reference program's by a relative error of at most 0.018.
Values may be sent and summed in bfloat16 or wider, within the bound.
No kernel may reach another device: no remote copies, remote signals or barrier semaphores. Data moves between devices by JAX's collectives and lax.ppermute only.
A program may use at most 128 MiB of HBM per device.

```python
import math
import jax
import jax.numpy as jnp
import numpy as np
from jax import lax

D = 768
HEADS = 12
HEAD = 64
FF = 3072
LAYERS = 1
DOCS = 4
TOK_DEV = 128
SEQUENCES = 32
TOKENS = 4096


def strengthened(array, own_key, source, target, blocks, factor):
    owner, partner = [(jnp.arange(array.shape[axis_at]) // (array.shape[axis_at] // blocks)).reshape([-1 if axis == axis_at else 1 for axis in range(array.ndim)]) for axis_at in (source, target)]
    chosen = jax.random.permutation(own_key, blocks)[partner]
    strong = (owner == chosen) | (owner == (partner + blocks // 2) % blocks)
    return jnp.where(strong, factor * array, array)


def block_levels(rng, shape, cuts, least, top_value):
    def one(axis_at, parts):
        steps = jax.random.uniform(jax.random.fold_in(jax.random.fold_in(rng, 6), axis_at), (parts,), jnp.float32, least / len(cuts), top_value / len(cuts))
        return jnp.repeat(jnp.exp(steps), shape[axis_at] // parts).reshape((-1,) + (1,) * (len(shape) - axis_at - 1))

    level = one(*cuts[0])
    for cut in cuts[1:]:
        level = level * one(*cut)
    return level


def profile(amount, total, limit, slope):
    loads = [(1 << 20) // math.isqrt(rank ** slope) + 1 for rank in range(2, amount + 1)]
    rest, counts = total - limit - (amount - 1), [1] * (amount - 1)
    while rest > 0:
        movable = [i for i in range(amount - 1) if counts[i] < limit]
        mass, remaining = sum([loads[i] for i in movable]), rest
        for i in movable:
            more = min(limit - counts[i], max(1, remaining * loads[i] // mass), rest)
            counts[i] = counts[i] + more
            rest = rest - more
    return np.array([limit] + counts)


def uneven_parts(stream_key, number_of, total, bound, skew):
    if number_of == 2:
        one = jax.random.randint(stream_key, (), max(1, total - bound), min(bound, total - 1) + 1)
        return jnp.stack([one, total - one])
    tallies = jnp.asarray(profile(number_of, total, bound, skew), jnp.int32)
    twos = (number_of - 1) // 2
    source_of, sink = tallies[1:1 + 2 * twos:2], tallies[2:2 + 2 * twos:2]
    margin = jnp.minimum(source_of - 1, bound - sink)
    moved = jax.random.randint(jax.random.fold_in(stream_key, 1), (twos,), 0, 1 << 20) % (margin + 1)
    tallies = tallies.at[1:1 + 2 * twos:2].set(source_of - moved).at[2:2 + 2 * twos:2].set(sink + moved)
    return tallies[jax.random.permutation(jax.random.fold_in(stream_key, 2), number_of)]


def normal_values(stream_key, shape, deviation, limit, shards=(), dtype=jnp.bfloat16):
    array = jax.random.normal(stream_key, shape, jnp.float32) * deviation
    if len(shards) > 0:
        array = block_levels(stream_key, shape, shards, -0.22, 0.18) * array
    return jnp.clip(array, min=-limit, max=limit).astype(dtype)


def gaussian_with(rng, dims, scale, bound, pieces, heavy, held_as=jnp.bfloat16):
    values = scale * jax.random.normal(rng, dims, jnp.float32)
    if pieces:
        values = values * block_levels(rng, dims, pieces, -0.22, 0.18)
    return jnp.clip(strengthened(values, jax.random.fold_in(rng, 3), *heavy), -bound, bound).astype(held_as)


def setup_inputs(seed: int = 0) -> dict:
    key_of = jax.random.split(jax.random.key(seed), 17)
    return {
        "hidden_in": gaussian_with(key_of[0], (TOKENS, D), 1.0, 6.0, ((0, 32),), (0, 1, 32, 2.75), jnp.float32),
        "doc_ids": jax.vmap(lambda own: jnp.searchsorted(jnp.cumsum(uneven_parts(own, DOCS, TOK_DEV, TOK_DEV // 2, 0)), jnp.arange(TOK_DEV), side="right"))(jax.random.split(key_of[1], SEQUENCES)).reshape((SEQUENCES, TOK_DEV)).astype(jnp.int32),
        "cotangent": normal_values(key_of[2], (TOKENS, D), 1.0, 6.0, ((0, 32),), jnp.float32),
        "pre_gain": jnp.clip(1.0 + 0.15 * jax.random.normal(key_of[3], (LAYERS, D), jnp.float32), 0.25, 1.75),
        "pre_shift": normal_values(key_of[4], (LAYERS, D), 0.5, 3.0, ((1, 8),), jnp.float32),
        "qkv_weight": normal_values(key_of[5], (LAYERS, D, 3 * D), D ** -0.5, 0.21875, ((1, 8),), jnp.float32),
        "query_bias": normal_values(key_of[6], (LAYERS, D), 0.5, 3.0, ((1, 8),), jnp.float32),
        "value_bias": normal_values(key_of[7], (LAYERS, D), 0.5, 3.0, ((1, 8),), jnp.float32),
        "out_weight": normal_values(key_of[8], (LAYERS, D, D), (D // 16) ** -0.5, 0.875, ((1, 8),), jnp.float32),
        "out_bias": normal_values(key_of[9], (LAYERS, D), 0.5, 3.0, ((1, 8),), jnp.float32),
        "post_gain": jnp.clip(1.0 + 0.15 * jax.random.normal(key_of[10], (LAYERS, D), jnp.float32), 0.25, 1.75),
        "post_shift": normal_values(key_of[11], (LAYERS, D), 0.5, 3.0, ((1, 8),), jnp.float32),
        "up_weight": normal_values(key_of[12], (LAYERS, D, FF), D ** -0.5, 0.21875, ((1, 8),), jnp.float32),
        "up_bias": normal_values(key_of[13], (LAYERS, FF), 0.5, 3.0, ((1, 8),), jnp.float32),
        "down_weight": normal_values(key_of[14], (LAYERS, FF, D), FF ** -0.5, 0.109375, ((1, 8),), jnp.float32),
        "down_bias": normal_values(key_of[15], (LAYERS, D), 0.5, 3.0, ((1, 8),), jnp.float32),
    }


@jax.custom_vjp
def low(v):
    return lax.optimization_barrier(v.astype(jnp.bfloat16)).astype(jnp.float32)

@jax.custom_vjp
def low_back(v):
    return v

def low_keep(v):
    return (low(v), None)

def low_pass(kept, grad):
    return (grad,)

def back_keep(v):
    return (v, None)

def back_low(kept, grad):
    return (low(grad),)
low.defvjp(low_keep, low_pass)
low_back.defvjp(back_keep, back_low)
EPS = 1e-05
GELU_C = 0.7978845608028654
NEG_FILL = -1e+30

def matmul(left, right):
    return jnp.dot(left, right, precision=lax.Precision.HIGHEST, preferred_element_type=jnp.float32)

def norm(values_in, gains, shifts):
    average = lax.optimization_barrier(jnp.mean(values_in, axis=-1, keepdims=True))
    centred = values_in - average
    spread = lax.optimization_barrier(jnp.mean(centred * centred, axis=-1, keepdims=True))
    return centred * lax.rsqrt(spread + EPS) * gains + shifts

def gelu_tanh(values_in):
    return 0.5 * values_in * (1.0 + jnp.tanh(GELU_C * (values_in + 0.044715 * values_in * values_in * values_in)))

def attend(group_in):
    queries, key_rows, value_rows, doc_rows = group_in
    product = jnp.einsum('gqhe,gkhe->ghqk', queries, key_rows, precision=lax.Precision.HIGHEST)
    scores = low_back(0.125 * product)
    length = doc_rows.shape[1]
    places = jnp.arange(length)
    causal = places[:, None] >= places[None, :]
    allowed = causal[None, None] & (doc_rows[:, None, :, None] == doc_rows[:, None, None, :])
    scores = jnp.where(allowed, scores, NEG_FILL)
    weights = low(jax.nn.softmax(scores, axis=-1))
    return jnp.einsum('ghqk,gkhe->gqhe', weights, value_rows, precision=lax.Precision.HIGHEST)

def block_forward(hidden, params, doc_ids):
    rounded = jax.tree.map(low, params)
    pre_gain, pre_shift, qkv_weight, query_bias, value_bias, out_weight, out_bias, post_gain, post_shift, up_weight, up_bias, down_weight, down_bias = rounded
    total_rows, width = hidden.shape
    seq_count, length = doc_ids.shape
    per_group = max(1, min(seq_count, 4096 // length))
    group_count = seq_count // per_group
    normed = low(norm(hidden, pre_gain, pre_shift))
    bias_row = jnp.concatenate([query_bias, jnp.zeros_like(query_bias), value_bias])
    packed = low(low_back(matmul(normed, qkv_weight) + bias_row))
    shaped = packed.reshape(group_count, per_group, length, 3, HEADS, HEAD)
    docs = doc_ids.reshape(group_count, per_group, length)
    mixed = lax.map(jax.checkpoint(attend), (shaped[:, :, :, 0], shaped[:, :, :, 1], shaped[:, :, :, 2], docs))
    mixed = low(low_back(mixed.reshape(total_rows, width)))
    middle = hidden + low_back(matmul(mixed, out_weight) + out_bias)
    normed_two = low(norm(middle, post_gain, post_shift))
    pre_act = low_back(matmul(normed_two, up_weight) + up_bias)
    activ = low(gelu_tanh(pre_act))
    return middle + low_back(matmul(activ, down_weight) + down_bias)

def reference(hidden_in, doc_ids, cotangent, pre_gain, pre_shift, qkv_weight, query_bias, value_bias, out_weight, out_bias, post_gain, post_shift, up_weight, up_bias, down_weight, down_bias):
    params = (pre_gain, pre_shift, qkv_weight, query_bias, value_bias, out_weight, out_bias, post_gain, post_shift, up_weight, up_bias, down_weight, down_bias)

    def forward(hidden, param_set):
        for layer_index in range(LAYERS):
            layer_params = tuple((stacked[layer_index] for stacked in param_set))
            hidden = block_forward(hidden, layer_params, doc_ids)
        return hidden
    output, pullback = jax.vjp(forward, hidden_in, params)
    input_grad, grads = pullback(cotangent)
    return (output, input_grad, grads[0], grads[1], grads[2], grads[3], grads[4], grads[5], grads[6], grads[7], grads[8], grads[9], grads[10], grads[11], grads[12])
```

```python
import jax
import jax.numpy as jnp
from jax import lax
from jax.experimental import pallas as pl
from jax.experimental.pallas import tpu as pltpu
from jax.sharding import PartitionSpec as P

HEADS = 12
HEAD = 64

EPS = 1e-05
GELU_C = 0.7978845608028654
NEG_FILL = -1e30
BF = jnp.bfloat16
F32 = jnp.float32


def mm(left, right):
    return jnp.dot(left, right, preferred_element_type=F32)


def mm_tn(left, right):
    return lax.dot_general(left, right, (((0,), (0,)), ((), ())), preferred_element_type=F32)


def mm_nt(left, right):
    return lax.dot_general(left, right, (((1,), (1,)), ((), ())), preferred_element_type=F32)


def norm_parts(rows):
    average = jnp.mean(rows, axis=-1, keepdims=True)
    centred = rows - average
    spread = jnp.mean(centred * centred, axis=-1, keepdims=True)
    scale = lax.rsqrt(spread + EPS)
    return centred * scale, scale


def norm_back(grad, unit, scale, gain):
    weighted = grad * gain
    return scale * (
        weighted
        - jnp.mean(weighted, axis=-1, keepdims=True)
        - unit * jnp.mean(weighted * unit, axis=-1, keepdims=True)
    )


def gelu_and_slope(f):
    t = jnp.tanh(GELU_C * (f + 0.044715 * f * f * f))
    value = 0.5 * f * (1.0 + t)
    slope = 0.5 * (1.0 + t) + 0.5 * f * (1.0 - t * t) * GELU_C * (1.0 + 3 * 0.044715 * f * f)
    return value, slope


def swap_by_index(blocks, index):
    blocks = list(blocks)
    bit = 1
    while bit < len(blocks):
        flag = (index & bit) > 0
        for low in range(len(blocks)):
            if low & bit == 0:
                first, second = blocks[low], blocks[low | bit]
                blocks[low] = jnp.where(flag, second, first)
                blocks[low | bit] = jnp.where(flag, first, second)
        bit *= 2
    return blocks


def group_size():
    size = lax.axis_size("rep")
    while HEADS % size:
        size //= 2
    return size


def to_rep(block, step):
    count = lax.axis_size("rep")
    return lax.ppermute(block, "rep", [(one, one ^ step) for one in range(count)])


def to_shard(block, step):
    count = lax.axis_size("shard")
    return lax.ppermute(block, "shard", [(one, one ^ step) for one in range(count)])


def to_side(block, level):
    reps, shards = lax.axis_size("rep"), lax.axis_size("shard")
    bits = group_size().bit_length() - 1
    pairs = []
    for one in range(reps):
        for place in range(shards):
            step = 1 << ((level + (place & 1)) % bits)
            pairs.append((one * shards + place, (one ^ step) * shards + place))
    return lax.ppermute(block, ("rep", "shard"), pairs)


def sides():
    return range(group_size().bit_length() - 1)


def gather_side(block):
    held = block[None]
    for level in sides():
        held = jnp.concatenate([held, to_side(held, level)], axis=0)
    return held


def reduce_side(low, high):
    total = low
    for level in reversed(sides()):
        if high is None:
            half = total.shape[0] // 2
            total, high = total[:half], total[half:].astype(BF)
        total = total + to_side(high, level).astype(F32)
        high = None
    return total[0]


def in_order(blocks, me):
    bits = group_size().bit_length() - 1
    core = lax.axis_index("shard") & 1
    if bits == 2:
        first, second = blocks[1], blocks[2]
        blocks = [blocks[0], jnp.where(core == 0, first, second),
                  jnp.where(core == 0, second, first), blocks[3]]
    return swap_by_index(blocks, me)


def from_order(blocks, me):
    bits = group_size().bit_length() - 1
    core = lax.axis_index("shard") & 1
    blocks = swap_by_index(blocks, me)
    if bits == 2:
        first, second = blocks[1], blocks[2]
        blocks = [blocks[0], jnp.where(core == 0, first, second),
                  jnp.where(core == 0, second, first), blocks[3]]
    return blocks


def exchange_side(blocks):
    held = jnp.stack(blocks)
    for level in sides():
        step = 1 << level
        pairs = held.reshape((-1, 2, step) + held.shape[1:])
        moved = to_side(pairs[:, 1], level)
        held = jnp.stack([pairs[:, 0], moved], axis=1).reshape(held.shape)
    return held


def after(block, *others):
    return lax.optimization_barrier((block,) + others)[0]


def place_kernel(at_ref, near_ref, far_ref, *out_refs):
    at = at_ref[0]
    for i in range(near_ref.shape[0]):
        for j, source in enumerate((near_ref, far_ref)):
            top = 0
            for out_ref in out_refs:
                rows, columns = out_ref.shape[1:]
                piece = source[i, top:top + rows, :columns]
                out_ref[at ^ (2 * i + j)] = piece.astype(out_ref.dtype)
                top += rows


def gather_links(block):
    count = lax.axis_size("shard") // 2
    return [block] + [to_shard(block, 2 * step) for step in range(1, count)]


def gather_pair(blocks, *parts):
    near = jnp.stack(blocks)
    far = to_shard(near, 1)
    place = lax.axis_index("shard").astype(jnp.int32).reshape(1)
    count = 2 * len(blocks)
    return pl.pallas_call(
        place_kernel,
        out_shape=[jax.ShapeDtypeStruct((count,) + shape, dtype) for shape, dtype in parts],
        in_specs=[pl.BlockSpec(memory_space=pltpu.SMEM), pl.BlockSpec(), pl.BlockSpec()],
    )(place, near, far)


def call(kernel, scalar, operands, outs):
    return pl.pallas_call(
        kernel,
        out_shape=[jax.ShapeDtypeStruct(shape, dtype) for shape, dtype in outs],
        in_specs=[pl.BlockSpec(memory_space=pltpu.SMEM)] + [pl.BlockSpec()] * len(operands),
    )(scalar, *operands)


def choose(index, pieces):
    out = pieces[0]
    for i in range(1, len(pieces)):
        out = jnp.where(index == i, pieces[i], out)
    return out


def pack_kernel(at_ref, w_ref, *refs):
    out_ref = refs[-1]
    rows = w_ref.shape[0]
    part = out_ref.shape[1] // 3
    ranks = w_ref.shape[1] // (3 * part)
    for j in range(3):
        first = j * ranks * part
        out_ref[0:rows, j * part:(j + 1) * part] = choose(
            at_ref[0], [w_ref[:, first + i * part:first + (i + 1) * part] for i in range(ranks)]
        ).astype(BF)
    lines = [ref[:, i:i + rows] for ref in refs[:-1] for i in range(0, ref.shape[1], rows)]
    out_ref[rows:rows + len(lines), 0:rows] = jnp.concatenate(lines, axis=0).astype(BF)


def pack_mlp_kernel(at_ref, up_ref, down_ref, out_ref):
    rows = up_ref.shape[0]
    hid = down_ref.shape[0]
    ranks = up_ref.shape[1] // (out_ref.shape[1] - down_ref.shape[1])
    part = hid // ranks
    for s in range(up_ref.shape[1] // hid):
        out_ref[:, s * part:(s + 1) * part] = choose(
            at_ref[0],
            [up_ref[:, s * hid + i * part:s * hid + (i + 1) * part] for i in range(ranks)]
        ).astype(BF)
    first = out_ref.shape[1] - down_ref.shape[1]
    out_ref[:, first:] = choose(
        at_ref[0], [down_ref[i * part:(i + 1) * part, :] for i in range(ranks)]).astype(BF)


def start_kernel(_, hidden_ref, cot_ref, docs_ref, out_ref):
    tokens, width = hidden_ref.shape
    out_ref[0:tokens] = norm_parts(hidden_ref[...])[0].astype(BF)
    out_ref[tokens:2 * tokens] = cot_ref[...].astype(BF)
    docs = docs_ref[...].astype(F32)
    line = jnp.concatenate([docs, jnp.zeros((1, width - tokens), F32)], axis=1)
    out_ref[2 * tokens:2 * tokens + 16] = jnp.broadcast_to(line, (16, width)).astype(BF)


def attend_kernel(_, all_ref, w_ref, gain_ref, shift_ref, bias_ref,
                  normed_ref, dm_ref, packed_ref, p_ref, out_ref):
    ranks, tokens, part = out_ref.shape
    heads = part // HEAD
    gain, shift = gain_ref[...], shift_ref[...]
    for g in range(ranks):
        span = slice(g * tokens, (g + 1) * tokens)
        normed_ref[span] = (all_ref[g, 0:tokens].astype(F32) * gain + shift).astype(BF)
        dm_ref[span] = all_ref[g, tokens:2 * tokens]
    packed_ref[...] = (mm(normed_ref[...], w_ref[...]) + bias_ref[...]).astype(BF)
    rows = lax.broadcasted_iota(jnp.int32, (tokens, tokens), 0)
    columns = lax.broadcasted_iota(jnp.int32, (tokens, tokens), 1)
    for g in range(ranks):
        span = slice(g * tokens, (g + 1) * tokens)
        line = all_ref[g, 2 * tokens:2 * tokens + 16, 0:tokens].astype(F32)[0:1]
        across = jnp.broadcast_to(line, (tokens, tokens))
        allowed = (rows >= columns) & (across == across.T)
        for h in range(heads):
            q = packed_ref[span, h * HEAD:(h + 1) * HEAD]
            k = packed_ref[span, part + h * HEAD:part + (h + 1) * HEAD]
            v = packed_ref[span, 2 * part + h * HEAD:2 * part + (h + 1) * HEAD]
            scores = jnp.where(allowed, mm_nt(q, k) * 0.125, NEG_FILL)
            powers = jnp.exp(scores - jnp.max(scores, axis=-1, keepdims=True))
            p = powers / jnp.sum(powers, axis=-1, keepdims=True)
            p_ref[g * heads + h] = p
            out_ref[g, :, h * HEAD:(h + 1) * HEAD] = mm(p.astype(BF), v).astype(BF)


def attend_back_kernel(at_ref, packed_ref, p_ref, do_ref, normed_ref, w_ref,
                       low_ref, high_ref, mine_ref, other_ref, sums_ref, grad_ref):
    ranks, tokens, part = do_ref.shape
    heads = part // HEAD
    for g in range(ranks):
        span = slice(g * tokens, (g + 1) * tokens)
        for h in range(heads):
            cq = slice(h * HEAD, (h + 1) * HEAD)
            ck = slice(part + h * HEAD, part + (h + 1) * HEAD)
            cv = slice(2 * part + h * HEAD, 2 * part + (h + 1) * HEAD)
            p = p_ref[g * heads + h]
            do = do_ref[g, :, cq]
            dp = mm_nt(do, packed_ref[span, cv])
            ds = (p * (dp - jnp.sum(dp * p, axis=-1, keepdims=True))).astype(BF)
            grad_ref[span, cv] = mm_tn(p.astype(BF), do).astype(BF)
            grad_ref[span, cq] = (mm(ds, packed_ref[span, ck]) * 0.125).astype(BF)
            grad_ref[span, ck] = (mm_tn(ds, packed_ref[span, cq]) * 0.125).astype(BF)
    grad = grad_ref[...]
    sums_ref[...] = jnp.sum(grad.astype(F32), axis=0, keepdims=True)
    split_rows(at_ref, mm_tn(normed_ref[...], grad), mine_ref, other_ref)
    half = ranks // 2
    for g in range(ranks):
        block = mm_nt(grad[g * tokens:(g + 1) * tokens], w_ref[...])
        if g < half:
            low_ref[g] = block
        else:
            high_ref[g - half] = block.astype(BF)


def split_rows(at_ref, whole, mine_ref, other_ref):
    rows = mine_ref.shape[1]
    even = at_ref[0] == 0
    for i in range(mine_ref.shape[0]):
        first = whole[2 * i * rows:(2 * i + 1) * rows]
        second = whole[(2 * i + 1) * rows:(2 * i + 2) * rows]
        mine_ref[i] = jnp.where(even, first, second)
        other_ref[i] = jnp.where(even, second, first).astype(BF)


def finish_kernel(at_ref, hidden_ref, grad_ref, middle_ref, gain_ref, bias_ref, hid_ref, rest_ref,
                  input_ref, mine_ref, other_ref):
    unit, scale = norm_parts(hidden_ref[...])
    grad = grad_ref[...]
    input_ref[...] = middle_ref[...] + norm_back(grad, unit, scale, gain_ref[...])
    width = grad.shape[1]
    part = bias_ref.shape[1] // 3
    ranks = width // part
    me, even = at_ref[1], at_ref[0] == 0

    def spread(first):
        piece = bias_ref[:, first:first + part]
        return jnp.concatenate(
            [jnp.where(me == i, piece, 0.0) for i in range(ranks)], axis=1)

    lines = [jnp.sum(grad * unit, axis=0, keepdims=True), jnp.sum(grad, axis=0, keepdims=True),
             spread(0), spread(2 * part), rest_ref[...]]
    lines = jnp.concatenate(lines, axis=0)
    hid = hid_ref[...]
    shards = 2 * mine_ref.shape[0]
    rows = width // shards
    per = hid.shape[1] // shards
    blocks = []
    for s in range(shards):
        own = jnp.concatenate(
            [jnp.where(me == i, hid[:, s * per:(s + 1) * per], 0.0) for i in range(ranks)], axis=1)
        own = [own[:, i:i + rows] for i in range(0, ranks * per, rows)]
        blocks.append(jnp.concatenate([lines[:, s * rows:(s + 1) * rows]] + own, axis=0))
    for i in range(mine_ref.shape[0]):
        mine_ref[i] = jnp.where(even, blocks[2 * i], blocks[2 * i + 1])
        other_ref[i] = jnp.where(even, blocks[2 * i + 1], blocks[2 * i]).astype(BF)


def split_shard(grad):
    shards = grad.shape[0]
    core = lax.axis_index("shard") & 1
    pairs = grad.reshape((shards // 2, 2) + grad.shape[1:])
    other = lax.dynamic_index_in_dim(pairs, core ^ 1, 1, keepdims=False)
    return lax.dynamic_index_in_dim(pairs, core, 1, keepdims=False), other.astype(BF)


def reduce_shard(mine, other):
    links = mine.shape[0]
    place = lax.axis_index("shard") >> 1
    mine = mine + to_shard(other, 1).astype(F32)
    total = lax.dynamic_index_in_dim(mine, place, 0, keepdims=False)
    mine = mine.astype(BF)
    for step in range(1, links):
        block = lax.dynamic_index_in_dim(mine, place ^ step, 0, keepdims=False)
        total = total + to_shard(block, 2 * step).astype(F32)
    step = group_size()
    while step < lax.axis_size("rep"):
        total = total + to_rep(total.astype(BF), step).astype(F32)
        step *= 2
    return total.astype(BF)


def split_plan(
    hidden, doc_ids, cotangent, pre_gain, pre_shift, qkv_weight, query_bias, value_bias,
    out_weight, out_bias, post_gain, post_shift, up_weight, up_bias, down_weight, down_bias,
):
    ranks = group_size()
    shards = lax.axis_size("shard")
    me = lax.axis_index("rep") & (ranks - 1)
    tokens, width = hidden.shape
    rows = qkv_weight.shape[1]
    part = width // ranks
    hid_rows = down_weight.shape[1]
    hid_part = hid_rows // ranks
    heads = HEADS // ranks

    core = lax.axis_index("shard") & 1
    at = jnp.stack([core, me]).astype(jnp.int32)
    mine = me.astype(jnp.int32).reshape(1)
    vectors = [pre_gain, pre_shift, query_bias, value_bias, out_bias, post_gain, post_shift,
               down_bias, up_bias]
    count = 8 + hid_rows // rows
    sent, = call(start_kernel, mine, (hidden, cotangent, doc_ids),
                 [((2 * tokens + 16, width), BF)])
    w_qkv, = call(pack_kernel, mine, [qkv_weight[0]] + vectors, [((rows + count, 3 * part), BF)])
    qkv_links = gather_links(w_qkv)
    every = gather_side(sent)
    w_qkv, vec = gather_pair(qkv_links, ((rows, 3 * part), BF), ((count, rows), F32))
    w_qkv = w_qkv.reshape(width, 3 * part)
    w_out = after(out_weight[0].astype(BF), *qkv_links)
    out_links = gather_links(w_out)
    w_out, = gather_pair(out_links, ((rows, width), BF))
    w_out = w_out.reshape(width, width)
    w_mlp, = call(pack_mlp_kernel, mine, (up_weight[0], down_weight[0]),
                  [((rows, shards * hid_part + width), BF)])
    mlp_links = gather_links(after(w_mlp, *out_links))
    w_mlp, = gather_pair(mlp_links, ((rows, shards * hid_part + width), BF))
    w_mlp = w_mlp.reshape(width, -1)
    w_up, w_down = w_mlp[:, :shards * hid_part], w_mlp[:, shards * hid_part:]

    lines = vec.transpose(1, 0, 2)
    p_gain, p_shift, q_bias, v_bias, o_bias, s_gain, s_shift, d_bias = [
        lines[i].reshape(1, width) for i in range(8)
    ]
    hid_bias = lines[8:].transpose(1, 0, 2).reshape(shards, ranks, hid_part)
    u_bias = lax.dynamic_index_in_dim(hid_bias, me, 1, keepdims=False).reshape(1, -1)

    def quarter(vector):
        return lax.dynamic_slice_in_dim(vector, me * part, part, 1)

    bias_row = jnp.concatenate([quarter(q_bias), jnp.zeros((1, part), F32), quarter(v_bias)], axis=1)
    whole = ranks * tokens
    normed_all, grad_down_all, packed, weights, mixed = call(
        attend_kernel, mine, (every, w_qkv, p_gain, p_shift, bias_row),
        [((whole, width), BF), ((whole, width), BF), ((whole, 3 * part), BF),
         ((ranks * heads, tokens, tokens), F32), ((ranks, tokens, part), BF)])
    mixed = exchange_side([mixed[i] for i in range(ranks)])
    mixed = jnp.concatenate(in_order([mixed[i] for i in range(ranks)], me), axis=1)
    middle = hidden + mm(mixed, w_out) + o_bias
    unit2, scale2 = norm_parts(middle)
    normed_two = (unit2 * s_gain + s_shift).astype(BF)
    normed_two_all = gather_side(normed_two).reshape(whole, width)
    pre_act = mm(normed_two_all, w_up) + u_bias
    activ, slope = gelu_and_slope(pre_act)
    activ = activ.astype(BF)

    half = ranks // 2
    grad_pre = (mm_nt(grad_down_all, w_down) * slope).astype(BF)
    sum_two = mm_nt(grad_pre, w_up).reshape(ranks, tokens, width)
    grad_two = reduce_side(sum_two[:half], sum_two[half:].astype(BF))
    g_s_gain = jnp.sum(grad_two * unit2, axis=0, keepdims=True)
    g_s_shift = jnp.sum(grad_two, axis=0, keepdims=True)
    grad_middle = cotangent + norm_back(grad_two, unit2, scale2, s_gain)
    grad_attn = grad_middle.astype(BF)
    grad_mixed = mm_nt(grad_attn, w_out).astype(BF)
    blocks = [grad_mixed[:, i * part:(i + 1) * part] for i in range(ranks)]
    grad_mixed = exchange_side(from_order(blocks, me))
    links = shards // 2
    low, high, qkv_mine, qkv_other, bias_sums, _ = call(
        attend_back_kernel, at, (packed, weights, grad_mixed, normed_all, w_qkv),
        [((half, tokens, width), F32), ((half, tokens, width), BF),
         ((links, rows, 3 * part), F32), ((links, rows, 3 * part), BF),
         ((1, 3 * part), F32), ((whole, 3 * part), BF)])
    grad_one = reduce_side(low, high)

    sum_out = mm(activ, w_down).reshape(ranks, tokens, width)
    hidden_out = reduce_side(sum_out[:half], sum_out[half:].astype(BF)) + (middle + d_bias)

    def by_shard(grad):
        return grad.reshape(shards, rows, -1)

    def every_rep(block):
        held = gather_side(block)
        return jnp.stack(in_order([held[i] for i in range(ranks)], me))

    g_mlp = reduce_shard(*split_shard(jnp.concatenate(
        [by_shard(mm_tn(normed_two_all, grad_pre)), by_shard(mm_tn(activ, grad_down_all))], axis=2)))
    g_mlp = every_rep(g_mlp)
    g_up = g_mlp[:, :, :shards * hid_part].astype(F32).reshape(ranks, rows, shards, hid_part)
    g_up = g_up.transpose(1, 2, 0, 3).reshape(1, rows, -1)
    g_down = g_mlp[:, :, shards * hid_part:].astype(F32).reshape(1, hid_rows, width)

    g_out = reduce_shard(*split_shard(by_shard(mm_tn(mixed, grad_attn))))
    g_out = jnp.sum(gather_side(g_out).astype(F32), axis=0)[None]

    g_qkv = every_rep(reduce_shard(qkv_mine, qkv_other)).astype(F32)
    g_qkv = g_qkv.reshape(ranks, rows, 3, part).transpose(1, 2, 0, 3).reshape(1, rows, -1)

    rest = jnp.concatenate([
        jnp.sum(grad_attn.astype(F32), axis=0, keepdims=True), g_s_gain, g_s_shift,
        jnp.sum(cotangent.astype(BF).astype(F32), axis=0, keepdims=True)], axis=0)
    hid_sums = jnp.sum(grad_pre.astype(F32), axis=0, keepdims=True)
    input_grad, sums_mine, sums_other = call(
        finish_kernel, at, (hidden, grad_one, grad_middle, p_gain, bias_sums, hid_sums, rest),
        [((tokens, width), F32), ((links, count, rows), F32), ((links, count, rows), BF)])
    sums = jnp.sum(gather_side(reduce_shard(sums_mine, sums_other)).astype(F32), axis=0)
    return (
        hidden_out, input_grad, sums[0:1], sums[1:2], g_qkv, sums[2:3], sums[3:4],
        g_out, sums[4:5], sums[5:6], sums[6:7], g_up, sums[8:].reshape(1, -1), g_down, sums[7:8],
    )


def solution(mesh):
    tokens = P(("rep", "shard"), None)
    vector = P(None, "shard")
    matrix = P(None, "shard", None)
    in_specs = (
        tokens, tokens, tokens, vector, vector, matrix, vector, vector, matrix, vector,
        vector, vector, matrix, vector, matrix, vector,
    )
    out_specs = (tokens, tokens) + in_specs[3:]
    return jax.shard_map(
        split_plan, mesh=mesh, in_specs=in_specs, out_specs=out_specs, check_vma=False
    )
```

```python
import jax
import jax.numpy as jnp
from jax import lax
from jax.experimental import pallas as pl
from jax.experimental.pallas import tpu as pltpu
from jax.sharding import PartitionSpec as P


HEADS = 12
HEAD = 64


EPS = 1e-05
GELU_C = 0.7978845608028654
NEG_FILL = -1e30
BF = jnp.bfloat16
F32 = jnp.float32


def mm(left, right):
    return jnp.dot(left, right, preferred_element_type=F32)


def mm_tn(left, right):
    return lax.dot_general(left, right, (((0,), (0,)), ((), ())), preferred_element_type=F32)


def mm_nt(left, right):
    return lax.dot_general(left, right, (((1,), (1,)), ((), ())), preferred_element_type=F32)


def norm_parts(rows):
    average = jnp.mean(rows, axis=-1, keepdims=True)
    centred = rows - average
    spread = jnp.mean(centred * centred, axis=-1, keepdims=True)
    scale = lax.rsqrt(spread + EPS)
    return centred * scale, scale


def norm_back(grad, unit, scale, gain):
    weighted = grad * gain
    return scale * (
        weighted
        - jnp.mean(weighted, axis=-1, keepdims=True)
        - unit * jnp.mean(weighted * unit, axis=-1, keepdims=True)
    )


def gelu_and_slope(f):
    t = jnp.tanh(GELU_C * (f + 0.044715 * f * f * f))
    value = 0.5 * f * (1.0 + t)
    slope = 0.5 * (1.0 + t) + 0.5 * f * (1.0 - t * t) * GELU_C * (1.0 + 3 * 0.044715 * f * f)
    return value, slope


def swap_by_index(blocks, index):
    blocks = list(blocks)
    bit = 1
    while bit < len(blocks):
        flag = (index & bit) > 0
        for low in range(len(blocks)):
            if low & bit == 0:
                first, second = blocks[low], blocks[low | bit]
                blocks[low] = jnp.where(flag, second, first)
                blocks[low | bit] = jnp.where(flag, first, second)
        bit *= 2
    return blocks


def group_size():
    size = lax.axis_size("rep")
    while HEADS % size:
        size //= 2
    return size


def to_rep(block, step):
    count = lax.axis_size("rep")
    return lax.ppermute(block, "rep", [(one, one ^ step) for one in range(count)])


def to_shard(block, step):
    count = lax.axis_size("shard")
    return lax.ppermute(block, "shard", [(one, one ^ step) for one in range(count)])


def to_side(block, level):
    reps, shards = lax.axis_size("rep"), lax.axis_size("shard")
    bits = group_size().bit_length() - 1
    pairs = []
    for one in range(reps):
        for place in range(shards):
            step = 1 << ((level + (place & 1)) % bits)
            pairs.append((one * shards + place, (one ^ step) * shards + place))
    return lax.ppermute(block, ("rep", "shard"), pairs)


def sides():
    return range(group_size().bit_length() - 1)


def gather_halves(block):
    held, moved = None, block[None]
    for level in sides():
        held = moved if held is None else jnp.concatenate([held, moved], axis=0)
        moved = to_side(held, level)
    return held, moved


def gather_side(block):
    return jnp.concatenate(gather_halves(block), axis=0)


def reduce_side(low, high):
    total = low
    for level in reversed(sides()):
        if high is None:
            half = total.shape[0] // 2
            total, high = total[:half], total[half:].astype(BF)
        moved = to_side(high, level)
        total = total + moved.astype(F32)
        high = None
    return total[0]


def in_order(blocks, me, core):
    if len(blocks) == 4:
        first, second = blocks[1], blocks[2]
        blocks = [blocks[0], jnp.where(core == 0, first, second),
                  jnp.where(core == 0, second, first), blocks[3]]
    return swap_by_index(blocks, me)


def from_order(blocks, me, core):
    blocks = swap_by_index(blocks, me)
    if len(blocks) == 4:
        first, second = blocks[1], blocks[2]
        blocks = [blocks[0], jnp.where(core == 0, first, second),
                  jnp.where(core == 0, second, first), blocks[3]]
    return blocks


def exchange_side(blocks):
    held = jnp.stack(blocks)
    for level in sides():
        step = 1 << level
        pairs = held.reshape((-1, 2, step) + held.shape[1:])
        moved = to_side(pairs[:, 1], level)
        held = jnp.stack([pairs[:, 0], moved], axis=1).reshape(held.shape)
    return held


def after(block, *others):
    return lax.optimization_barrier((block,) + others)[0]


def place_kernel(at_ref, near_ref, far_ref, *out_refs):
    at = at_ref[0]
    for i in range(near_ref.shape[0]):
        for j, source in enumerate((near_ref, far_ref)):
            top = 0
            for out_ref in out_refs:
                rows, columns = out_ref.shape[1:]
                piece = source[i, top:top + rows, :columns]
                out_ref[at ^ (2 * i + j)] = piece.astype(out_ref.dtype)
                top += rows


def gather_links(block):
    count = lax.axis_size("shard") // 2
    return [block] + [to_shard(block, 2 * step) for step in range(1, count)]


def gather_pair(blocks, *parts):
    near = jnp.stack(blocks)
    far = to_shard(near, 1)
    place = lax.axis_index("shard").astype(jnp.int32).reshape(1)
    count = 2 * len(blocks)
    return pl.pallas_call(
        place_kernel,
        out_shape=[jax.ShapeDtypeStruct((count,) + shape, dtype) for shape, dtype in parts],
        in_specs=[pl.BlockSpec(memory_space=pltpu.SMEM), pl.BlockSpec(), pl.BlockSpec()],
    )(place, near, far)


def call(kernel, scalar, operands, outs):
    return pl.pallas_call(
        kernel,
        out_shape=[jax.ShapeDtypeStruct(shape, dtype) for shape, dtype in outs],
        in_specs=[pl.BlockSpec(memory_space=pltpu.SMEM)] + [pl.BlockSpec()] * len(operands),
    )(scalar, *operands)


def choose(index, pieces):
    out = pieces[0]
    for i in range(1, len(pieces)):
        out = jnp.where(index == i, pieces[i], out)
    return out


def pack_kernel(at_ref, w_ref, *refs):
    out_ref = refs[-1]
    rows = w_ref.shape[0]
    part = out_ref.shape[1] // 3
    ranks = w_ref.shape[1] // (3 * part)
    for j in range(3):
        first = j * ranks * part
        out_ref[0:rows, j * part:(j + 1) * part] = choose(
            at_ref[0], [w_ref[:, first + i * part:first + (i + 1) * part] for i in range(ranks)]
        ).astype(BF)
    lines = [ref[:, i:i + rows] for ref in refs[:-1] for i in range(0, ref.shape[1], rows)]
    out_ref[rows:rows + len(lines), 0:rows] = jnp.concatenate(lines, axis=0).astype(BF)


def pack_mlp_kernel(at_ref, up_ref, down_ref, out_ref):
    hid = down_ref.shape[0]
    ranks = up_ref.shape[1] // (out_ref.shape[1] - down_ref.shape[1])
    part = hid // ranks
    for s in range(up_ref.shape[1] // hid):
        out_ref[:, s * part:(s + 1) * part] = choose(
            at_ref[0],
            [up_ref[:, s * hid + i * part:s * hid + (i + 1) * part] for i in range(ranks)]
        ).astype(BF)
    first = out_ref.shape[1] - down_ref.shape[1]
    out_ref[:, first:] = choose(
        at_ref[0], [down_ref[i * part:(i + 1) * part, :] for i in range(ranks)]).astype(BF)


def start_kernel(_, hidden_ref, cot_ref, docs_ref, out_ref):
    tokens, width = hidden_ref.shape
    out_ref[0:tokens] = norm_parts(hidden_ref[...])[0].astype(BF)
    out_ref[tokens:2 * tokens] = cot_ref[...].astype(BF)
    docs = docs_ref[...].astype(F32)
    line = jnp.concatenate([docs, jnp.zeros((1, width - tokens), F32)], axis=1)
    out_ref[2 * tokens:2 * tokens + 16] = jnp.broadcast_to(line, (16, width)).astype(BF)


def attend_kernel(at_ref, low_ref, high_ref, w_ref, vec_ref,
                  normed_ref, dm_ref, packed_ref, p_ref, out_ref, lines_ref, hid_ref):
    ranks, tokens, part = out_ref.shape
    heads = part // HEAD
    shards, count, rows = vec_ref.shape
    me = at_ref[0]
    lines = jnp.concatenate([vec_ref[s] for s in range(shards)], axis=1)
    lines_ref[...] = lines[0:8]
    hid_ref[...] = choose(me, [lines[8 + i:9 + i] for i in range(count - 8)])
    gain, shift = lines[0:1], lines[1:2]
    bias = [choose(me, [lines[j:j + 1, i * part:(i + 1) * part] for i in range(ranks)])
            for j in (2, 3)]
    bias = jnp.concatenate([bias[0], jnp.zeros((1, part), F32), bias[1]], axis=1)
    sources = [ref.at[i] for ref in (low_ref, high_ref) for i in range(ranks // 2)]
    for g in range(ranks):
        span = slice(g * tokens, (g + 1) * tokens)
        normed_ref[span] = (sources[g][0:tokens].astype(F32) * gain + shift).astype(BF)
        dm_ref[span] = sources[g][tokens:2 * tokens]
    packed_ref[...] = (mm(normed_ref[...], w_ref[...]) + bias).astype(BF)
    rows = lax.broadcasted_iota(jnp.int32, (tokens, tokens), 0)
    columns = lax.broadcasted_iota(jnp.int32, (tokens, tokens), 1)
    for g in range(ranks):
        span = slice(g * tokens, (g + 1) * tokens)
        line = sources[g][2 * tokens:2 * tokens + 16, 0:tokens].astype(F32)[0:1]
        across = jnp.broadcast_to(line, (tokens, tokens))
        allowed = (rows >= columns) & (across == across.T)
        for h in range(heads):
            q = packed_ref[span, h * HEAD:(h + 1) * HEAD]
            k = packed_ref[span, part + h * HEAD:part + (h + 1) * HEAD]
            v = packed_ref[span, 2 * part + h * HEAD:2 * part + (h + 1) * HEAD]
            scores = jnp.where(allowed, mm_nt(q, k) * 0.125, NEG_FILL)
            powers = jnp.exp(scores - jnp.max(scores, axis=-1, keepdims=True))
            p = powers / jnp.sum(powers, axis=-1, keepdims=True)
            p_ref[g * heads + h] = p
            out_ref[g, :, h * HEAD:(h + 1) * HEAD] = mm(p.astype(BF), v).astype(BF)


def attend_back_kernel(at_ref, packed_ref, p_ref, do_ref, normed_ref, w_ref,
                       low_ref, high_ref, mine_ref, other_ref, sums_ref, grad_ref):
    ranks, tokens, part = do_ref.shape
    heads = part // HEAD
    for g in range(ranks):
        span = slice(g * tokens, (g + 1) * tokens)
        for h in range(heads):
            cq = slice(h * HEAD, (h + 1) * HEAD)
            ck = slice(part + h * HEAD, part + (h + 1) * HEAD)
            cv = slice(2 * part + h * HEAD, 2 * part + (h + 1) * HEAD)
            p = p_ref[g * heads + h]
            do = do_ref[g, :, cq]
            dp = mm_nt(do, packed_ref[span, cv])
            ds = (p * (dp - jnp.sum(dp * p, axis=-1, keepdims=True))).astype(BF)
            grad_ref[span, cv] = mm_tn(p.astype(BF), do).astype(BF)
            grad_ref[span, cq] = (mm(ds, packed_ref[span, ck]) * 0.125).astype(BF)
            grad_ref[span, ck] = (mm_tn(ds, packed_ref[span, cq]) * 0.125).astype(BF)
    grad = grad_ref[...]
    sums_ref[...] = jnp.sum(grad.astype(F32), axis=0, keepdims=True)
    split_rows(at_ref, mm_tn(normed_ref[...], grad), mine_ref, other_ref)
    half = ranks // 2
    for g in range(ranks):
        block = mm_nt(grad[g * tokens:(g + 1) * tokens], w_ref[...])
        if g < half:
            low_ref[g] = block
        else:
            high_ref[g - half] = block.astype(BF)


def split_rows(at_ref, whole, mine_ref, other_ref):
    rows = mine_ref.shape[1]
    even = at_ref[0] == 0
    for i in range(mine_ref.shape[0]):
        first = whole[2 * i * rows:(2 * i + 1) * rows]
        second = whole[(2 * i + 1) * rows:(2 * i + 2) * rows]
        mine_ref[i] = jnp.where(even, first, second)
        other_ref[i] = jnp.where(even, second, first).astype(BF)


def unpack_qkv_kernel(at_ref, low_ref, high_ref, out_ref):
    half, _, columns = low_ref.shape
    part = columns // 3
    blocks = [ref[i] for ref in (low_ref, high_ref) for i in range(half)]
    blocks = in_order(blocks, at_ref[1], at_ref[0])
    out_ref[...] = jnp.concatenate(
        [one[:, j * part:(j + 1) * part].astype(F32) for j in range(3) for one in blocks], axis=1)


def unpack_mlp_kernel(at_ref, low_ref, high_ref, up_ref, down_ref):
    half, _, columns = low_ref.shape
    width = down_ref.shape[1]
    ranks = 2 * half
    per = down_ref.shape[0] // ranks
    blocks = [ref[i] for ref in (low_ref, high_ref) for i in range(half)]
    blocks = in_order(blocks, at_ref[1], at_ref[0])
    for r, one in enumerate(blocks):
        down_ref[r * per:(r + 1) * per] = one[:, columns - width:].astype(F32)
    for s in range((columns - width) // per):
        up_ref[:, s * ranks * per:(s + 1) * ranks * per] = jnp.concatenate(
            [one[:, s * per:(s + 1) * per].astype(F32) for one in blocks], axis=1)


def finish_kernel(at_ref, hidden_ref, grad_ref, middle_ref, gain_ref, bias_ref, hid_ref, rest_ref,
                  input_ref, mine_ref, other_ref):
    unit, scale = norm_parts(hidden_ref[...])
    grad = grad_ref[...]
    input_ref[...] = middle_ref[...] + norm_back(grad, unit, scale, gain_ref[...])
    width = grad.shape[1]
    part = bias_ref.shape[1] // 3
    ranks = width // part
    me, even = at_ref[1], at_ref[0] == 0

    def spread(first):
        piece = bias_ref[:, first:first + part]
        return jnp.concatenate(
            [jnp.where(me == i, piece, 0.0) for i in range(ranks)], axis=1)

    lines = [jnp.sum(grad * unit, axis=0, keepdims=True), jnp.sum(grad, axis=0, keepdims=True),
             spread(0), spread(2 * part), rest_ref[...]]
    lines = jnp.concatenate(lines, axis=0)
    hid = hid_ref[...]
    shards = 2 * mine_ref.shape[0]
    rows = width // shards
    per = hid.shape[1] // shards
    blocks = []
    for s in range(shards):
        own = jnp.concatenate(
            [jnp.where(me == i, hid[:, s * per:(s + 1) * per], 0.0) for i in range(ranks)], axis=1)
        own = [own[:, i:i + rows] for i in range(0, ranks * per, rows)]
        blocks.append(jnp.concatenate([lines[:, s * rows:(s + 1) * rows]] + own, axis=0))
    for i in range(mine_ref.shape[0]):
        mine_ref[i] = jnp.where(even, blocks[2 * i], blocks[2 * i + 1])
        other_ref[i] = jnp.where(even, blocks[2 * i + 1], blocks[2 * i]).astype(BF)


def split_shard(grad):
    shards = grad.shape[0]
    core = lax.axis_index("shard") & 1
    pairs = grad.reshape((shards // 2, 2) + grad.shape[1:])
    other = lax.dynamic_index_in_dim(pairs, core ^ 1, 1, keepdims=False)
    return lax.dynamic_index_in_dim(pairs, core, 1, keepdims=False), other.astype(BF)


def reduce_shard(mine, other):
    links = mine.shape[0]
    place = lax.axis_index("shard") >> 1
    moved = to_shard(other, 1)
    mine = mine + moved.astype(F32)
    total = lax.dynamic_index_in_dim(mine, place, 0, keepdims=False)
    mine = mine.astype(BF)
    for step in range(1, links):
        block = lax.dynamic_index_in_dim(mine, place ^ step, 0, keepdims=False)
        moved = to_shard(block, 2 * step)
        total = total + moved.astype(F32)
    step = group_size()
    while step < lax.axis_size("rep"):
        total = total + to_rep(total.astype(BF), step).astype(F32)
        step *= 2
    return total.astype(BF)


def split_plan(
    hidden, doc_ids, cotangent, pre_gain, pre_shift, qkv_weight, query_bias, value_bias,
    out_weight, out_bias, post_gain, post_shift, up_weight, up_bias, down_weight, down_bias,
):
    ranks = group_size()
    shards = lax.axis_size("shard")
    me = lax.axis_index("rep") & (ranks - 1)
    tokens, width = hidden.shape
    rows = qkv_weight.shape[1]
    part = width // ranks
    hid_rows = down_weight.shape[1]
    hid_part = hid_rows // ranks
    heads = HEADS // ranks

    core = lax.axis_index("shard") & 1
    at = jnp.stack([core, me]).astype(jnp.int32)
    mine = me.astype(jnp.int32).reshape(1)
    vectors = [pre_gain, pre_shift, query_bias, value_bias, out_bias, post_gain, post_shift,
               down_bias, up_bias]
    count = 8 + hid_rows // rows
    sent, = call(start_kernel, mine, (hidden, cotangent, doc_ids),
                 [((2 * tokens + 16, width), BF)])
    lines = -(-(rows + count) // 16) * 16
    w_qkv, = call(pack_kernel, mine, [qkv_weight[0]] + vectors, [((lines, 3 * part), BF)])
    qkv_links = gather_links(w_qkv)
    every_low, every_high = gather_halves(sent)
    w_qkv, vec = gather_pair(qkv_links, ((rows, 3 * part), BF), ((count, rows), F32))
    w_qkv = w_qkv.reshape(width, 3 * part)
    w_out = after(out_weight[0].astype(BF), *qkv_links)
    out_links = gather_links(w_out)
    w_out, = gather_pair(out_links, ((rows, width), BF))
    w_out = w_out.reshape(width, width)
    w_mlp, = call(pack_mlp_kernel, mine, (up_weight[0], down_weight[0]),
                  [((rows, shards * hid_part + width), BF)])
    whole = ranks * tokens
    normed_all, grad_down_all, packed, weights, mixed, lines, u_bias = call(
        attend_kernel, mine, (every_low, every_high, w_qkv, vec),
        [((whole, width), BF), ((whole, width), BF), ((whole, 3 * part), BF),
         ((ranks * heads, tokens, tokens), F32), ((ranks, tokens, part), BF),
         ((8, width), F32), ((1, shards * hid_part), F32)])
    p_gain, _, _, _, o_bias, s_gain, s_shift, d_bias = [lines[i:i + 1] for i in range(8)]
    mlp_links = gather_links(after(w_mlp, w_qkv))
    mixed = exchange_side([mixed[i] for i in range(ranks)])
    mixed = jnp.concatenate(in_order([mixed[i] for i in range(ranks)], me, core), axis=1)
    middle = hidden + mm(mixed, w_out) + o_bias
    unit2, scale2 = norm_parts(middle)
    normed_two = (unit2 * s_gain + s_shift).astype(BF)
    two_low, two_high = gather_halves(normed_two)
    normed_two_all = jnp.concatenate([two_low, two_high], axis=0).reshape(whole, width)
    mlp_links = lax.optimization_barrier((*mlp_links, two_low))[:-1]
    w_mlp, = gather_pair(mlp_links, ((rows, shards * hid_part + width), BF))
    w_mlp = w_mlp.reshape(width, -1)
    w_up, w_down = w_mlp[:, :shards * hid_part], w_mlp[:, shards * hid_part:]
    pre_act = mm(normed_two_all, w_up) + u_bias
    activ, slope = gelu_and_slope(pre_act)
    activ = activ.astype(BF)

    half = ranks // 2
    grad_pre = (mm_nt(grad_down_all, w_down) * slope).astype(BF)
    sum_two = mm_nt(grad_pre, w_up).reshape(ranks, tokens, width)
    grad_two = reduce_side(sum_two[:half], sum_two[half:].astype(BF))
    g_s_gain = jnp.sum(grad_two * unit2, axis=0, keepdims=True)
    g_s_shift = jnp.sum(grad_two, axis=0, keepdims=True)
    grad_middle = cotangent + norm_back(grad_two, unit2, scale2, s_gain)
    grad_attn = grad_middle.astype(BF)
    grad_mixed = mm_nt(grad_attn, w_out).astype(BF)
    blocks = [grad_mixed[:, i * part:(i + 1) * part] for i in range(ranks)]
    grad_mixed = exchange_side(from_order(blocks, me, core))
    links = shards // 2
    low, high, qkv_mine, qkv_other, bias_sums, _ = call(
        attend_back_kernel, at, (packed, weights, grad_mixed, normed_all, w_qkv),
        [((half, tokens, width), F32), ((half, tokens, width), BF),
         ((links, rows, 3 * part), F32), ((links, rows, 3 * part), BF),
         ((1, 3 * part), F32), ((whole, 3 * part), BF)])
    grad_one = reduce_side(low, high)

    sum_out = mm(activ, w_down).reshape(ranks, tokens, width)
    hidden_out = reduce_side(
        sum_out[:half], after(sum_out[half:].astype(BF), grad_mixed)) + (middle + d_bias)

    def by_shard(grad):
        return grad.reshape(shards, rows, -1)

    g_mlp = reduce_shard(*split_shard(jnp.concatenate(
        [by_shard(mm_tn(normed_two_all, grad_pre)), by_shard(mm_tn(activ, grad_down_all))], axis=2)))
    g_mlp = gather_halves(g_mlp)
    g_up, g_down = call(
        unpack_mlp_kernel, at, g_mlp,
        [((rows, ranks * shards * hid_part), F32), ((hid_rows, width), F32)])
    g_up, g_down = g_up[None], g_down[None]

    g_out = reduce_shard(*split_shard(by_shard(mm_tn(mixed, grad_attn))))
    g_out = jnp.sum(gather_side(g_out).astype(F32), axis=0)[None]

    g_qkv = gather_halves(reduce_shard(qkv_mine, qkv_other))
    g_qkv, = call(unpack_qkv_kernel, at, g_qkv, [((rows, 3 * width), F32)])
    g_qkv = g_qkv[None]

    rest = jnp.concatenate([
        jnp.sum(grad_attn.astype(F32), axis=0, keepdims=True), g_s_gain, g_s_shift,
        jnp.sum(cotangent.astype(BF).astype(F32), axis=0, keepdims=True)], axis=0)
    hid_sums = jnp.sum(grad_pre.astype(F32), axis=0, keepdims=True)
    input_grad, sums_mine, sums_other = call(
        finish_kernel, at, (hidden, grad_one, grad_middle, p_gain, bias_sums, hid_sums, rest),
        [((tokens, width), F32), ((links, count, rows), F32), ((links, count, rows), BF)])
    sums = jnp.sum(gather_side(reduce_shard(sums_mine, sums_other)).astype(F32), axis=0)
    return (
        hidden_out, input_grad, sums[0:1], sums[1:2], g_qkv, sums[2:3], sums[3:4],
        g_out, sums[4:5], sums[5:6], sums[6:7], g_up, sums[8:].reshape(1, -1), g_down, sums[7:8],
    )


def solution(mesh):
    tokens = P(("rep", "shard"), None)
    vector = P(None, "shard")
    matrix = P(None, "shard", None)
    in_specs = (
        tokens, tokens, tokens, vector, vector, matrix, vector, vector, matrix, vector,
        vector, vector, matrix, vector, matrix, vector,
    )
    out_specs = (tokens, tokens) + in_specs[3:]

    return jax.shard_map(
        split_plan, mesh=mesh, in_specs=in_specs, out_specs=out_specs, check_vma=False
    )
```
